32 devices in a mesh: ctx: 8 (over y, x, core), ch: 4 (over z).
Axes of the slice: x: 2, y: 2, z: 4, core: 2. Of those that a mesh axis runs over, the one named last changes fastest.
Arguments:
- query_gate: bfloat16 [2048, 4096], P('ctx', 'ch'), may hold values from -6 to 6
- key_gate: bfloat16 [2048, 4096], P('ctx', 'ch'), may hold values from -6 to 6
- values: bfloat16 [2048, 4096], P('ctx', 'ch'), may hold values from -6 to 6
- decay_rates: float32 [16, 4096], P(None, 'ch'), may hold values from 0 to 0.04, as said below
- residues: float32 [16, 4096], P(None, 'ch'), may hold values from -3 to 3
- skip_gain: float32 [4096], P('ch'), may hold values from 0.5 to 1.5
- out_weight: bfloat16 [4096, 4096], P(None, 'ch'), may hold values from -0.09375 to 0.09375
Outputs:
- layer_out: bfloat16 [2048, 4096], P('ctx', 'ch')
- final_state: float32 [16, 4096], P(None, ('ctx', 'ch'))
The draws below stay inside these ranges and needn't reach their ends.
Inputs may be any that keep to these rules, and one draw needn't show every extreme that they name: `decay_rates`: decay rates are positive.
All inputs are finite; a program needn't handle non-finite values.
Results may differ from the reference program's by a relative error of at most 0.0057.
Values may be sent and summed in bfloat16 or wider, within the bound.
A program may use at most 192 MiB of HBM per device.

```python
import jax
import jax.numpy as jnp
from jax import lax

D = 4096
M = 16
SEQ = 2048


def draw_decay_rates(key, part):
    first = jax.random.fold_in(key, 0)
    return jnp.exp(jax.random.uniform(first, (M, D), jnp.float32, jnp.log(2.0 / SEQ), jnp.log(1.0 / 30.0)))


def levels(key, shape, pieces, least, high):
    gain, own = 1.0, jax.random.fold_in(key, 6)
    for position, blocks in pieces:
        steps = jnp.exp(jax.random.uniform(jax.random.fold_in(own, position), (blocks,), jnp.float32, least / len(pieces), high / len(pieces)))
        gain = gain * jnp.repeat(steps, shape[position] // blocks).reshape([-1 if axis == position else 1 for axis in range(len(shape))])
    return gain


def scatter_about(key, shape, spread, limit, cuts=(), held_as=jnp.bfloat16):
    values = spread * jax.random.normal(key, shape, jnp.float32)
    if cuts:
        values = values * levels(key, shape, cuts, -0.22, 0.18)
    return jnp.clip(values, -limit, limit).astype(held_as)


def setup_inputs(seed: int = 0) -> dict:
    keys = jax.random.split(jax.random.key(seed), 8)
    return {
        "query_gate": scatter_about(keys[0], (SEQ, D), 1.0, 6.0, ((0, 8), (1, 4))),
        "key_gate": scatter_about(keys[1], (SEQ, D), 1.0, 6.0, ((0, 8), (1, 4))),
        "values": scatter_about(keys[2], (SEQ, D), 1.0, 6.0, ((0, 8), (1, 4))),
        "decay_rates": draw_decay_rates(jax.random.fold_in(keys[7], 71), 0),
        "residues": scatter_about(keys[4], (M, D), 0.35, 3.0, ((1, 4),), jnp.float32),
        "skip_gain": jnp.clip(0.5 + 1.0 * jax.random.uniform(keys[5], (D,), jnp.float32) ** levels(keys[5], (D,), ((0, 4),), -0.2, 0.2), 0.5, 1.5),
        "out_weight": scatter_about(keys[6], (D, D), D ** -0.5, 0.09375, ((1, 4),)),
    }


def reference(query_gate, key_gate, values, decay_rates, residues, skip_gain, out_weight):
    gated = (key_gate.astype(jnp.float32) * values.astype(jnp.float32)).astype(jnp.bfloat16)
    amplitude = residues * jnp.sqrt(-jnp.expm1(-2.0 * decay_rates))
    signal = gated.astype(jnp.float32)
    length = signal.shape[0]
    channels = signal.shape[1]
    group = 128
    group_count = channels // group
    sig_groups = signal.reshape(length, group_count, group).transpose(1, 0, 2)
    rate_groups = decay_rates.reshape(M, group_count, group).transpose(1, 0, 2)
    amp_groups = amplitude.reshape(M, group_count, group).transpose(1, 0, 2)
    skip_groups = skip_gain.reshape(group_count, group)
    positions = jnp.arange(length).astype(jnp.float32)

    def one_group(packed):
        sig_part, rate_part, amp_part, skip_part = packed

        def add_mode(acc, pair):
            rate_row, amp_row = pair
            taps = acc + amp_row[None, :] * jnp.exp(-rate_row[None, :] * positions[:, None])
            tail = lax.optimization_barrier(jnp.sum(jnp.exp(-rate_row[None, :] * (length - 1.0 - positions)[:, None]) * sig_part, axis=0))
            return (taps, tail)
        taps, tails = lax.scan(add_mode, jnp.zeros((length, group), jnp.float32), (rate_part, amp_part))
        spectrum = jnp.fft.rfft(sig_part, n=2 * length, axis=0) * jnp.fft.rfft(taps, n=2 * length, axis=0)
        convolved = jnp.fft.irfft(spectrum, n=2 * length, axis=0)[:length]
        convolved = convolved + skip_part[None, :] * sig_part
        return (convolved, tails * amp_part)
    conv_groups, final_groups = lax.map(one_group, (sig_groups, rate_groups, amp_groups, skip_groups))
    convolved = conv_groups.transpose(1, 0, 2).reshape(length, channels)
    final_state = final_groups.transpose(1, 0, 2).reshape(M, channels)
    mixing = (query_gate.astype(jnp.float32) * convolved).astype(jnp.bfloat16)
    layer_out = jnp.dot(mixing, out_weight, preferred_element_type=jnp.float32).astype(jnp.bfloat16)
    return (layer_out, final_state)
```

```python
import functools

import jax
import jax.numpy as jnp
from jax import lax
from jax.experimental import pallas as pl
from jax.experimental.pallas import tpu as pltpu
from jax.sharding import PartitionSpec as P

LANES = 128
SEGS = 8
CHUNK = 256
MESH = pl.DeviceIdType.MESH


def one_minus_exp(z):
    series = 1.0 - z * (1.0 / 8.0)
    for k in (7.0, 6.0, 5.0, 4.0, 3.0, 2.0):
        series = 1.0 - z * (1.0 / k) * series
    return jnp.where(z < 0.25, z * series, 1.0 - jnp.exp(-z))


def kernel(
    ctx_count, groups, chunk, fin_width, fin_stride,
    q_hbm, k_hbm, v_hbm, rate_ref, res_ref, skip_ref, w_hbm,
    out_ref, fin_ref,
    qb, kb, vb, wb, ub, yb, qp, mix, acc, states, seed_in, seed_pow, inc, final_row, final_got,
    perm, perm_back,
    load_sem, w_sem, st_send, st_recv, mx_send, mx_recv, fin_send, fin_recv,
):
    rows, channels = qb.shape
    poles = rate_ref.shape[0]
    steps = rows // SEGS
    chunks = channels // chunk
    tiles = chunk // LANES
    me = lax.axis_index("ctx")
    here = lax.axis_index("ch")

    loads = []
    for c in range(chunks):
        sl = pl.ds(c * chunk, chunk)
        group = []
        for n, (src, dst) in enumerate(((k_hbm, kb), (v_hbm, vb), (q_hbm, qb))):
            copy = pltpu.make_async_copy(src.at[:, sl], dst.at[:, sl], load_sem.at[n, c])
            copy.start()
            group.append(copy)
        loads.append(group)
    w_copy = pltpu.make_async_copy(w_hbm, wb, w_sem)
    w_copy.start()

    barrier = pltpu.get_barrier_semaphore()
    for d in range(1, ctx_count):
        pl.semaphore_signal(
            barrier, inc=1, device_id={"ctx": lax.rem(me + d, ctx_count)}, device_id_type=MESH
        )
    for d in range(1, groups):
        pl.semaphore_signal(
            barrier, inc=1, device_id={"ch": lax.rem(here + d, groups)}, device_id_type=MESH
        )

    first = lax.broadcasted_iota(jnp.int32, (rows, rows), 0)
    second = lax.broadcasted_iota(jnp.int32, (rows, rows), 1)
    perm[...] = jnp.where(second == (first % SEGS) * steps + first // SEGS, 1.0, 0.0).astype(jnp.bfloat16)
    perm_back[...] = jnp.where(first == (second % SEGS) * steps + second // SEGS, 1.0, 0.0).astype(jnp.bfloat16)

    def spread(ref, lane):
        return jnp.stack(
            [jnp.broadcast_to(ref[m : m + 1, pl.ds(lane, LANES)], (SEGS, LANES)) for m in range(poles)]
        )

    seg = lax.broadcasted_iota(jnp.int32, (poles, SEGS, LANES), 1)

    def state_copy(slot, peer, c):
        sl = pl.ds(c * chunk, chunk)
        return pltpu.make_async_remote_copy(
            src_ref=states.at[slot, :, sl],
            dst_ref=states.at[slot, :, sl],
            send_sem=st_send.at[peer, c],
            recv_sem=st_recv.at[slot, c],
            device_id={"ctx": peer},
            device_id_type=MESH,
        )

    for c in range(chunks):
        sl = pl.ds(c * chunk, chunk)
        for copy in loads[c]:
            copy.wait()
        gated = (kb[:, sl].astype(jnp.float32) * vb[:, sl].astype(jnp.float32)).astype(jnp.bfloat16)
        ub[:, sl] = jnp.dot(perm[...], gated, preferred_element_type=jnp.float32)

        @pl.loop(0, tiles)
        def _(t):
            lane = pl.multiple_of(c * chunk + t * LANES, LANES)
            tl = pl.ds(lane, LANES)
            rate = spread(rate_ref, lane)
            amp = spread(res_ref, lane) * jnp.sqrt(one_minus_exp(2.0 * rate))
            pole = jnp.exp(-rate)
            skip = jnp.broadcast_to(skip_ref[0:1, tl], (SEGS, LANES))

            def step(i, x):
                at = pl.ds(pl.multiple_of(i * SEGS, SEGS), SEGS)
                u = ub[at, tl]
                x = pole * x + u[None]
                yb[at, tl] = jnp.sum(amp * x, axis=0) + skip * u
                return x

            x = lax.fori_loop(0, steps, step, jnp.zeros((poles, SEGS, LANES), jnp.float32), unroll=4)
            span = 1
            while span < SEGS:
                weight = jnp.where(seg >= span, jnp.exp(rate * (-1.0 * steps * span)), 0.0)
                x = x + weight * pltpu.roll(x, span, 1)
                span *= 2
            for m in range(poles):
                states[me, m : m + 1, tl] = x[m, SEGS - 1 : SEGS]
            before = jnp.where(seg >= 1, pltpu.roll(x, 1, 1), 0.0)
            seed_in[:, :, tl] = amp * before
            seed_pow[:, :, tl] = amp * jnp.exp(rate * (seg.astype(jnp.float32) * (-1.0 * steps)))

        if c == 0:
            pl.semaphore_wait(barrier, ctx_count - 1 + groups - 1)
        for d in range(1, ctx_count):
            state_copy(me, lax.rem(me + d, ctx_count), c).start()

    for c in range(chunks):
        sl = pl.ds(c * chunk, chunk)
        qp[:, sl] = jnp.dot(perm[...], qb[:, sl], preferred_element_type=jnp.float32)

    def mix_copy(owner, c, way):
        sl = pl.ds(pl.multiple_of(c * chunk, chunk), chunk)
        return pltpu.make_async_remote_copy(
            src_ref=mix.at[owner, :, sl],
            dst_ref=mix.at[owner, :, sl],
            send_sem=mx_send.at[way, owner, c],
            recv_sem=mx_recv.at[owner, c],
            device_id={"ch": here + 1 if way else here - 1},
            device_id_type=MESH,
        )

    has_right = here < groups - 1
    has_left = here > 0

    for c in range(chunks):
        sl = pl.ds(c * chunk, chunk)
        for d in range(1, ctx_count):
            state_copy(lax.rem(me + d, ctx_count), me, c).wait_recv()
        rate = rate_ref[:, sl]
        across = jnp.exp(rate * (-1.0 * rows))
        total = jnp.zeros_like(rate)
        incoming = jnp.zeros_like(rate)
        for j in range(ctx_count):
            incoming = jnp.where(me == j, total, incoming)
            total = total * across + states[j, :, sl]
        inc[:, sl] = incoming
        final_row[:, sl] = res_ref[:, sl] * jnp.sqrt(one_minus_exp(2.0 * rate)) * total

        @pl.loop(0, tiles)
        def _(t):
            lane = pl.multiple_of(c * chunk + t * LANES, LANES)
            tl = pl.ds(lane, LANES)
            pole = jnp.exp(-spread(rate_ref, lane))
            carry = seed_in[:, :, tl] + seed_pow[:, :, tl] * spread(inc, lane)

            def step(i, x):
                at = pl.ds(pl.multiple_of(i * SEGS, SEGS), SEGS)
                x = pole * x
                yb[at, tl] += jnp.sum(x, axis=0)
                return x

            lax.fori_loop(0, steps, step, carry, unroll=4)

        mixing = (qp[:, sl] * yb[:, sl]).astype(jnp.bfloat16)
        mix[here, :, sl] = jnp.dot(
            perm_back[...], mixing, preferred_element_type=jnp.float32
        ).astype(jnp.bfloat16)

        @pl.when(has_right)
        def _():
            mix_copy(here, c, 1).start()

        @pl.when(has_left)
        def _():
            mix_copy(here, c, 0).start()

    root = me * groups // ctx_count
    first_col = lax.rem(me * groups, ctx_count) * (channels // ctx_count)

    def final_copy(peer):
        return pltpu.make_async_remote_copy(
            src_ref=final_row.at[:, pl.ds(pl.multiple_of(first_col + peer * fin_stride, LANES), fin_width)],
            dst_ref=final_got,
            send_sem=fin_send.at[peer],
            recv_sem=fin_recv,
            device_id={"ch": peer},
            device_id_type=MESH,
        )

    @pl.when(here == root)
    def _():
        for d in range(1, groups):
            final_copy(lax.rem(here + d, groups)).start()

    w_copy.wait()

    def project(owner, c):
        at = pl.multiple_of(c * chunk, chunk)
        return jnp.dot(
            mix[owner, :, pl.ds(at, chunk)],
            wb[pl.ds(pl.multiple_of(owner * channels + at, chunk), chunk), :],
            preferred_element_type=jnp.float32,
        )

    acc[...] = project(here, 0)
    if chunks > 1:
        @pl.loop(1, chunks)
        def _(c):
            acc[...] += project(here, c)

    @pl.loop(0, (groups - 1) * chunks)
    def _(n):
        d = 1 + n // chunks
        c = n % chunks
        left = here - d
        right = here + d

        @pl.when(left >= 0)
        def _():
            mix_copy(left, c, 1).wait_recv()

            @pl.when(has_right)
            def _():
                mix_copy(left, c, 1).start()

        @pl.when(right < groups)
        def _():
            mix_copy(right, c, 0).wait_recv()

            @pl.when(has_left)
            def _():
                mix_copy(right, c, 0).start()

        @pl.when(left >= 0)
        def _():
            acc[...] += project(left, c)

        @pl.when(right < groups)
        def _():
            acc[...] += project(right, c)

    out_ref[...] = acc[...].astype(jnp.bfloat16)

    @pl.when(here == root)
    def _():
        fin_ref[...] = final_row[:, pl.ds(pl.multiple_of(first_col + here * fin_stride, LANES), fin_width)]
        for d in range(1, groups):
            final_copy(lax.rem(here + d, groups)).wait_send()

    @pl.when(here != root)
    def _():
        final_copy(here).wait_recv()
        fin_ref[...] = final_got[...]

    for c in range(chunks):
        for d in range(1, ctx_count):
            state_copy(me, lax.rem(me + d, ctx_count), c).wait_send()

    @pl.loop(0, groups * chunks)
    def _(n):
        owner = n // chunks
        c = n % chunks

        @pl.when(jnp.logical_and(owner <= here, has_right))
        def _():
            mix_copy(owner, c, 1).wait_send()

        @pl.when(jnp.logical_and(owner >= here, has_left))
        def _():
            mix_copy(owner, c, 0).wait_send()


def body(query_gate, key_gate, values, decay_rates, residues, skip_gain, out_weight):
    rows, channels = values.shape
    poles = decay_rates.shape[0]
    ctx_count = lax.axis_size("ctx")
    groups = lax.axis_size("ch")
    chunk = min(CHUNK, channels)
    chunks = channels // chunk
    columns = out_weight.shape[1]
    slice_width = channels // ctx_count
    aligned = slice_width % LANES == 0
    fin_width = slice_width if aligned else groups * slice_width
    fin_stride = slice_width if aligned else 0
    f32, bf16 = jnp.float32, jnp.bfloat16
    dma = pltpu.SemaphoreType.DMA
    any_spec = pl.BlockSpec(memory_space=pl.ANY)
    vmem = pl.BlockSpec(memory_space=pltpu.VMEM)
    layer_out, final = pl.pallas_call(
        functools.partial(kernel, ctx_count, groups, chunk, fin_width, fin_stride),
        out_shape=(
            jax.ShapeDtypeStruct((rows, columns), bf16),
            jax.ShapeDtypeStruct((poles, fin_width), f32),
        ),
        in_specs=[any_spec, any_spec, any_spec, vmem, vmem, vmem, any_spec],
        out_specs=(vmem, vmem),
        scratch_shapes=[
            pltpu.VMEM((rows, channels), bf16),
            pltpu.VMEM((rows, channels), bf16),
            pltpu.VMEM((rows, channels), bf16),
            pltpu.VMEM(out_weight.shape, bf16),
            pltpu.VMEM((rows, channels), f32),
            pltpu.VMEM((rows, channels), f32),
            pltpu.VMEM((rows, channels), f32),
            pltpu.VMEM((groups, rows, channels), bf16),
            pltpu.VMEM((rows, columns), f32),
            pltpu.VMEM((ctx_count, poles, channels), f32),
            pltpu.VMEM((poles, SEGS, channels), f32),
            pltpu.VMEM((poles, SEGS, channels), f32),
            pltpu.VMEM((poles, channels), f32),
            pltpu.VMEM((poles, channels), f32),
            pltpu.VMEM((poles, fin_width), f32),
            pltpu.VMEM((rows, rows), bf16),
            pltpu.VMEM((rows, rows), bf16),
            dma((3, chunks)),
            dma,
            dma((ctx_count, chunks)),
            dma((ctx_count, chunks)),
            dma((2, groups, chunks)),
            dma((groups, chunks)),
            dma((groups,)),
            dma,
        ],
        compiler_params=pltpu.CompilerParams(
            collective_id=0, has_side_effects=True, vmem_limit_bytes=60 * 1024 * 1024
        ),
    )(query_gate, key_gate, values, decay_rates, residues, skip_gain[None, :], out_weight)
    if not aligned:
        final = lax.dynamic_slice_in_dim(final, lax.axis_index("ch") * slice_width, slice_width, 1)
    return layer_out, final


def solution(mesh):
    return jax.shard_map(
        body,
        mesh=mesh,
        in_specs=(
            P("ctx", "ch"),
            P("ctx", "ch"),
            P("ctx", "ch"),
            P(None, "ch"),
            P(None, "ch"),
            P("ch"),
            P(None, "ch"),
        ),
        out_specs=(P("ctx", "ch"), P(None, ("ctx", "ch"))),
        check_vma=False,
    )
```

```python
import functools

import jax
import jax.numpy as jnp
from jax import lax
from jax.experimental import pallas as pl
from jax.experimental.pallas import tpu as pltpu
from jax.sharding import PartitionSpec as P

LANES = 128
SEGS = 8
CHUNK = 256
AHEAD = 3
MESH = pl.DeviceIdType.MESH


def one_minus_exp(z):
    series = 1.0 - z * (1.0 / 8.0)
    for k in (7.0, 6.0, 5.0, 4.0, 3.0, 2.0):
        series = 1.0 - z * (1.0 / k) * series
    return jnp.where(z < 0.25, z * series, 1.0 - jnp.exp(-z))


def kernel(
    ctx_count, groups, chunk, fin_width, fin_stride,
    q_hbm, k_hbm, v_hbm, rate_ref, res_ref, skip_ref, w_hbm,
    out_ref, fin_ref,
    qb, kb, vb, wb, ub, yb, qp, mix, acc, states, seed_in, seed_pow, inc, final_row, final_got,
    perm, perm_back,
    load_sem, w_sem, st_send, st_recv, mx_send, mx_recv, fin_send, fin_recv,
):
    rows, channels = qb.shape
    poles = rate_ref.shape[0]
    steps = rows // SEGS
    chunks = channels // chunk
    tiles = chunk // LANES
    me = lax.axis_index("ctx")
    here = lax.axis_index("ch")

    loads = []
    for c in range(chunks):
        sl = pl.ds(c * chunk, chunk)
        group = []
        for n, (src, dst) in enumerate(((k_hbm, kb), (v_hbm, vb), (q_hbm, qb))):
            copy = pltpu.make_async_copy(src.at[:, sl], dst.at[:, sl], load_sem.at[n, c])
            copy.start()
            group.append(copy)
        loads.append(group)
    w_copy = pltpu.make_async_copy(w_hbm, wb, w_sem)
    w_copy.start()

    barrier = pltpu.get_barrier_semaphore()
    for d in range(1, ctx_count):
        pl.semaphore_signal(
            barrier, inc=1, device_id={"ctx": lax.rem(me + d, ctx_count)}, device_id_type=MESH
        )
    for d in range(1, groups):
        pl.semaphore_signal(
            barrier, inc=1, device_id={"ch": lax.rem(here + d, groups)}, device_id_type=MESH
        )

    first = lax.broadcasted_iota(jnp.int32, (rows, rows), 0)
    second = lax.broadcasted_iota(jnp.int32, (rows, rows), 1)
    perm[...] = jnp.where(second == (first & (SEGS - 1)) * steps + (first >> 3), 1.0, 0.0).astype(jnp.bfloat16)
    perm_back[...] = jnp.where(first == (second & (SEGS - 1)) * steps + (second >> 3), 1.0, 0.0).astype(jnp.bfloat16)

    def spread(ref, lane):
        return jnp.stack(
            [jnp.broadcast_to(ref[m : m + 1, pl.ds(lane, LANES)], (SEGS, LANES)) for m in range(poles)]
        )

    seg = lax.broadcasted_iota(jnp.int32, (poles, SEGS, LANES), 1)

    def state_copy(slot, peer, c):
        return pltpu.make_async_remote_copy(
            src_ref=states.at[slot, c],
            dst_ref=states.at[slot, c],
            send_sem=st_send.at[peer, c],
            recv_sem=st_recv.at[slot, c],
            device_id={"ctx": peer},
            device_id_type=MESH,
        )

    def local(c):
        sl = pl.ds(c * chunk, chunk)
        for copy in loads[c]:
            copy.wait()
        gated = (kb[:, sl].astype(jnp.float32) * vb[:, sl].astype(jnp.float32)).astype(jnp.bfloat16)
        ub[:, sl] = jnp.dot(perm[...], gated, preferred_element_type=jnp.float32)

        @pl.loop(0, tiles)
        def _(t):
            lane = pl.multiple_of(c * chunk + t * LANES, LANES)
            tl = pl.ds(lane, LANES)
            rate = spread(rate_ref, lane)
            amp = spread(res_ref, lane) * jnp.sqrt(one_minus_exp(2.0 * rate))
            pole = jnp.exp(-rate)
            skip = jnp.broadcast_to(skip_ref[0:1, tl], (SEGS, LANES))

            def step(i, x):
                at = pl.ds(pl.multiple_of(i * SEGS, SEGS), SEGS)
                u = ub[at, tl]
                x = pole * x + u[None]
                yb[at, tl] = jnp.sum(amp * x, axis=0) + skip * u
                return x

            x = lax.fori_loop(0, steps, step, jnp.zeros((poles, SEGS, LANES), jnp.float32), unroll=4)
            span = 1
            while span < SEGS:
                weight = jnp.where(seg >= span, jnp.exp(rate * (-1.0 * steps * span)), 0.0)
                x = x + weight * pltpu.roll(x, span, 1)
                span *= 2
            for m in range(poles):
                states[me, c, m : m + 1, pl.ds(pl.multiple_of(t * LANES, LANES), LANES)] = x[m, SEGS - 1 : SEGS]
            before = jnp.where(seg >= 1, pltpu.roll(x, 1, 1), 0.0)
            seed_in[:, :, tl] = amp * before
            seed_pow[:, :, tl] = amp * jnp.exp(rate * (seg.astype(jnp.float32) * (-1.0 * steps)))

        if c == 0:
            pl.semaphore_wait(barrier, ctx_count - 1 + groups - 1)
        for d in range(1, ctx_count):
            state_copy(me, lax.rem(me + d, ctx_count), c).start()
        qp[:, sl] = jnp.dot(perm[...], qb[:, sl], preferred_element_type=jnp.float32)

    def mix_copy(owner, c, way):
        return pltpu.make_async_remote_copy(
            src_ref=mix.at[owner, c],
            dst_ref=mix.at[owner, c],
            send_sem=mx_send.at[way, owner, c],
            recv_sem=mx_recv.at[owner, c],
            device_id={"ch": here + 1 if way else here - 1},
            device_id_type=MESH,
        )

    has_right = here < groups - 1
    has_left = here > 0

    def finish(c):
        sl = pl.ds(c * chunk, chunk)
        for d in range(1, ctx_count):
            state_copy(lax.rem(me + d, ctx_count), me, c).wait_recv()
        rate = rate_ref[:, sl]
        across = jnp.exp(rate * (-1.0 * rows))
        total = jnp.zeros_like(rate)
        incoming = jnp.zeros_like(rate)
        for j in range(ctx_count):
            incoming = jnp.where(me == j, total, incoming)
            total = total * across + states[j, c]
        inc[:, sl] = incoming
        final_row[:, sl] = res_ref[:, sl] * jnp.sqrt(one_minus_exp(2.0 * rate)) * total

        @pl.loop(0, tiles)
        def _(t):
            lane = pl.multiple_of(c * chunk + t * LANES, LANES)
            tl = pl.ds(lane, LANES)
            pole = jnp.exp(-spread(rate_ref, lane))
            carry = seed_in[:, :, tl] + seed_pow[:, :, tl] * spread(inc, lane)

            def step(i, x):
                at = pl.ds(pl.multiple_of(i * SEGS, SEGS), SEGS)
                x = pole * x
                yb[at, tl] += jnp.sum(x, axis=0)
                return x

            lax.fori_loop(0, steps, step, carry, unroll=4)

        mixing = (qp[:, sl] * yb[:, sl]).astype(jnp.bfloat16)
        mix[here, c] = jnp.dot(
            perm_back[...], mixing, preferred_element_type=jnp.float32
        ).astype(jnp.bfloat16)

        @pl.when(has_right)
        def _():
            mix_copy(here, c, 1).start()

        @pl.when(has_left)
        def _():
            mix_copy(here, c, 0).start()

    for c in range(chunks + AHEAD):
        if c < chunks:
            local(c)
        if c >= AHEAD:
            finish(c - AHEAD)

    root = me * groups // ctx_count
    first_col = lax.rem(me * groups, ctx_count) * (channels // ctx_count)

    def final_copy(peer):
        return pltpu.make_async_remote_copy(
            src_ref=final_row.at[:, pl.ds(pl.multiple_of(first_col + peer * fin_stride, LANES), fin_width)],
            dst_ref=final_got,
            send_sem=fin_send.at[peer],
            recv_sem=fin_recv,
            device_id={"ch": peer},
            device_id_type=MESH,
        )

    @pl.when(here == root)
    def _():
        for d in range(1, groups):
            final_copy(lax.rem(here + d, groups)).start()

    w_copy.wait()

    def project(owner, c):
        at = pl.multiple_of(c * chunk, chunk)
        return jnp.dot(
            mix[owner, c],
            wb[pl.ds(pl.multiple_of(owner * channels + at, chunk), chunk), :],
            preferred_element_type=jnp.float32,
        )

    acc[...] = project(here, 0)
    if chunks > 1:
        @pl.loop(1, chunks)
        def _(c):
            acc[...] += project(here, c)

    @pl.loop(0, (groups - 1) * chunks)
    def _(n):
        d = 1 + n // chunks
        c = n % chunks
        left = here - d
        right = here + d

        @pl.when(left >= 0)
        def _():
            mix_copy(left, c, 1).wait_recv()

            @pl.when(has_right)
            def _():
                mix_copy(left, c, 1).start()

        @pl.when(right < groups)
        def _():
            mix_copy(right, c, 0).wait_recv()

            @pl.when(has_left)
            def _():
                mix_copy(right, c, 0).start()

        @pl.when(left >= 0)
        def _():
            acc[...] += project(left, c)

        @pl.when(right < groups)
        def _():
            acc[...] += project(right, c)

    out_ref[...] = acc[...].astype(jnp.bfloat16)

    @pl.when(here == root)
    def _():
        fin_ref[...] = final_row[:, pl.ds(pl.multiple_of(first_col + here * fin_stride, LANES), fin_width)]
        for d in range(1, groups):
            final_copy(lax.rem(here + d, groups)).wait_send()

    @pl.when(here != root)
    def _():
        final_copy(here).wait_recv()
        fin_ref[...] = final_got[...]

    for c in range(chunks):
        for d in range(1, ctx_count):
            state_copy(me, lax.rem(me + d, ctx_count), c).wait_send()

    @pl.loop(0, groups * chunks)
    def _(n):
        owner = n // chunks
        c = n % chunks

        @pl.when(jnp.logical_and(owner <= here, has_right))
        def _():
            mix_copy(owner, c, 1).wait_send()

        @pl.when(jnp.logical_and(owner >= here, has_left))
        def _():
            mix_copy(owner, c, 0).wait_send()


def write_out(out_ref, fin_ref, out_hbm, fin_hbm, sems):
    first = pltpu.make_async_copy(out_ref, out_hbm, sems.at[0])
    second = pltpu.make_async_copy(fin_ref, fin_hbm, sems.at[1])
    first.start()
    second.start()
    first.wait()
    second.wait()


def body(query_gate, key_gate, values, decay_rates, residues, skip_gain, out_weight):
    rows, channels = values.shape
    poles = decay_rates.shape[0]
    ctx_count = lax.axis_size("ctx")
    groups = lax.axis_size("ch")
    chunk = min(CHUNK, channels)
    chunks = channels // chunk
    columns = out_weight.shape[1]
    slice_width = channels // ctx_count
    aligned = slice_width % LANES == 0
    fin_width = slice_width if aligned else groups * slice_width
    fin_stride = slice_width if aligned else 0
    f32, bf16 = jnp.float32, jnp.bfloat16
    dma = pltpu.SemaphoreType.DMA
    any_spec = pl.BlockSpec(memory_space=pl.ANY)
    vmem = pl.BlockSpec(memory_space=pltpu.VMEM)
    layer_out, final = pl.pallas_call(
        functools.partial(kernel, ctx_count, groups, chunk, fin_width, fin_stride),
        out_shape=(
            jax.ShapeDtypeStruct((rows, columns), bf16),
            jax.ShapeDtypeStruct((poles, fin_width), f32),
        ),
        in_specs=[any_spec, any_spec, any_spec, vmem, vmem, vmem, any_spec],
        out_specs=(vmem, vmem),
        scratch_shapes=[
            pltpu.VMEM((rows, channels), bf16),
            pltpu.VMEM((rows, channels), bf16),
            pltpu.VMEM((rows, channels), bf16),
            pltpu.VMEM(out_weight.shape, bf16),
            pltpu.VMEM((rows, channels), f32),
            pltpu.VMEM((rows, channels), f32),
            pltpu.VMEM((rows, channels), f32),
            pltpu.VMEM((groups, chunks, rows, chunk), bf16),
            pltpu.VMEM((rows, columns), f32),
            pltpu.VMEM((ctx_count, chunks, poles, chunk), f32),
            pltpu.VMEM((poles, SEGS, channels), f32),
            pltpu.VMEM((poles, SEGS, channels), f32),
            pltpu.VMEM((poles, channels), f32),
            pltpu.VMEM((poles, channels), f32),
            pltpu.VMEM((poles, fin_width), f32),
            pltpu.VMEM((rows, rows), bf16),
            pltpu.VMEM((rows, rows), bf16),
            dma((3, chunks)),
            dma,
            dma((ctx_count, chunks)),
            dma((ctx_count, chunks)),
            dma((2, groups, chunks)),
            dma((groups, chunks)),
            dma((groups,)),
            dma,
        ],
        compiler_params=pltpu.CompilerParams(
            collective_id=0, has_side_effects=True, vmem_limit_bytes=60 * 1024 * 1024
        ),
    )(query_gate, key_gate, values, decay_rates, residues, skip_gain[None, :], out_weight)
    layer_out, final = pl.pallas_call(
        write_out,
        out_shape=(
            jax.ShapeDtypeStruct(layer_out.shape, layer_out.dtype),
            jax.ShapeDtypeStruct(final.shape, final.dtype),
        ),
        in_specs=[vmem, vmem],
        out_specs=(any_spec, any_spec),
        scratch_shapes=[dma((2,))],
    )(layer_out, final)
    if not aligned:
        final = lax.dynamic_slice_in_dim(final, lax.axis_index("ch") * slice_width, slice_width, 1)
    return layer_out, final


def solution(mesh):
    return jax.shard_map(
        body,
        mesh=mesh,
        in_specs=(
            P("ctx", "ch"),
            P("ctx", "ch"),
            P("ctx", "ch"),
            P(None, "ch"),
            P(None, "ch"),
            P("ch"),
            P(None, "ch"),
        ),
        out_specs=(P("ctx", "ch"), P(None, ("ctx", "ch"))),
        check_vma=False,
    )
```

```python
import functools

import jax
import jax.numpy as jnp
from jax import lax
from jax.experimental import pallas as pl
from jax.experimental.pallas import tpu as pltpu
from jax.sharding import PartitionSpec as P

LANES = 128
SEGS = 8
CHUNK = 256
AHEAD = 1
MESH = pl.DeviceIdType.MESH


def one_minus_exp(z):
    series = 1.0 - z * (1.0 / 8.0)
    for k in (7.0, 6.0, 5.0, 4.0, 3.0, 2.0):
        series = 1.0 - z * (1.0 / k) * series
    return jnp.where(z < 0.25, z * series, 1.0 - jnp.exp(-z))


def kernel(
    ctx_count, groups, chunk, fin_width, fin_stride,
    q_hbm, k_hbm, v_hbm, rate_ref, res_ref, skip_ref, w_hbm,
    out_ref, fin_ref,
    qb, kb, vb, wb, ub, yb, qp, mix, acc, states, seed_in, seed_pow, inc, final_row, final_got,
    perm, perm_back,
    load_sem, w_sem, st_send, st_recv, mx_send, mx_recv, fin_send, fin_recv,
):
    rows, channels = qb.shape
    poles = rate_ref.shape[0]
    steps = rows // SEGS
    chunks = channels // chunk
    tiles = chunk // LANES
    me = lax.axis_index("ctx")
    here = lax.axis_index("ch")

    loads = []
    for c in range(chunks):
        sl = pl.ds(c * chunk, chunk)
        group = []
        for n, (src, dst) in enumerate(((k_hbm, kb), (v_hbm, vb), (q_hbm, qb))):
            copy = pltpu.make_async_copy(src.at[:, sl], dst.at[:, sl], load_sem.at[n, c])
            copy.start()
            group.append(copy)
        loads.append(group)
    w_copy = pltpu.make_async_copy(w_hbm, wb, w_sem)

    barrier = pltpu.get_barrier_semaphore()
    for d in range(1, ctx_count):
        pl.semaphore_signal(
            barrier, inc=1, device_id={"ctx": lax.rem(me + d, ctx_count)}, device_id_type=MESH
        )
    for d in range(1, groups):
        pl.semaphore_signal(
            barrier, inc=1, device_id={"ch": lax.rem(here + d, groups)}, device_id_type=MESH
        )

    first = lax.broadcasted_iota(jnp.int32, (rows, rows), 0)
    second = lax.broadcasted_iota(jnp.int32, (rows, rows), 1)
    perm[...] = jnp.where(second == (first & (SEGS - 1)) * steps + (first >> 3), 1.0, 0.0).astype(jnp.bfloat16)
    perm_back[...] = jnp.where(first == (second & (SEGS - 1)) * steps + (second >> 3), 1.0, 0.0).astype(jnp.bfloat16)

    def spread(ref, lane):
        return jnp.stack(
            [jnp.broadcast_to(ref[m : m + 1, pl.ds(lane, LANES)], (SEGS, LANES)) for m in range(poles)]
        )

    seg = lax.broadcasted_iota(jnp.int32, (poles, SEGS, LANES), 1)

    def state_copy(slot, peer, c):
        return pltpu.make_async_remote_copy(
            src_ref=states.at[slot, c],
            dst_ref=states.at[slot, c],
            send_sem=st_send.at[peer, c],
            recv_sem=st_recv.at[slot, c],
            device_id={"ctx": peer},
            device_id_type=MESH,
        )

    def local(c):
        sl = pl.ds(c * chunk, chunk)
        for copy in loads[c]:
            copy.wait()
        if c == 0:
            w_copy.start()
        gated = (kb[:, sl].astype(jnp.float32) * vb[:, sl].astype(jnp.float32)).astype(jnp.bfloat16)
        ub[:, sl] = jnp.dot(perm[...], gated, preferred_element_type=jnp.float32)

        @pl.loop(0, tiles)
        def _(t):
            lane = pl.multiple_of(c * chunk + t * LANES, LANES)
            tl = pl.ds(lane, LANES)
            rate = spread(rate_ref, lane)
            amp = spread(res_ref, lane) * jnp.sqrt(one_minus_exp(2.0 * rate))
            pole = jnp.exp(-rate)
            skip = jnp.broadcast_to(skip_ref[0:1, tl], (SEGS, LANES))

            def step(i, x):
                at = pl.ds(pl.multiple_of(i * SEGS, SEGS), SEGS)
                u = ub[at, tl]
                x = pole * x + u[None]
                yb[at, tl] = jnp.sum(amp * x, axis=0) + skip * u
                return x

            x = lax.fori_loop(0, steps, step, jnp.zeros((poles, SEGS, LANES), jnp.float32), unroll=4)
            span = 1
            while span < SEGS:
                weight = jnp.where(seg >= span, jnp.exp(rate * (-1.0 * steps * span)), 0.0)
                x = x + weight * pltpu.roll(x, span, 1)
                span *= 2
            for m in range(poles):
                states[me, c, m : m + 1, pl.ds(pl.multiple_of(t * LANES, LANES), LANES)] = x[m, SEGS - 1 : SEGS]
            before = jnp.where(seg >= 1, pltpu.roll(x, 1, 1), 0.0)
            seed_in[:, :, tl] = amp * before
            seed_pow[:, :, tl] = amp * jnp.exp(rate * (seg.astype(jnp.float32) * (-1.0 * steps)))

        if c == 0:
            pl.semaphore_wait(barrier, ctx_count - 1 + groups - 1)
        for d in range(1, ctx_count):
            state_copy(me, lax.rem(me + d, ctx_count), c).start()
        qp[:, sl] = jnp.dot(perm[...], qb[:, sl], preferred_element_type=jnp.float32)

    def mix_copy(owner, c, way):
        return pltpu.make_async_remote_copy(
            src_ref=mix.at[owner, c],
            dst_ref=mix.at[owner, c],
            send_sem=mx_send.at[way, owner, c],
            recv_sem=mx_recv.at[owner, c],
            device_id={"ch": here + 1 if way else here - 1},
            device_id_type=MESH,
        )

    has_right = here < groups - 1
    has_left = here > 0

    def finish(c):
        sl = pl.ds(c * chunk, chunk)
        for d in range(1, ctx_count):
            state_copy(lax.rem(me + d, ctx_count), me, c).wait_recv()
        rate = rate_ref[:, sl]
        across = jnp.exp(rate * (-1.0 * rows))
        total = jnp.zeros_like(rate)
        incoming = jnp.zeros_like(rate)
        for j in range(ctx_count):
            incoming = jnp.where(me == j, total, incoming)
            total = total * across + states[j, c]
        inc[:, sl] = incoming
        final_row[:, sl] = res_ref[:, sl] * jnp.sqrt(one_minus_exp(2.0 * rate)) * total

        @pl.loop(0, tiles)
        def _(t):
            lane = pl.multiple_of(c * chunk + t * LANES, LANES)
            tl = pl.ds(lane, LANES)
            pole = jnp.exp(-spread(rate_ref, lane))
            carry = seed_in[:, :, tl] + seed_pow[:, :, tl] * spread(inc, lane)

            def step(i, x):
                at = pl.ds(pl.multiple_of(i * SEGS, SEGS), SEGS)
                x = pole * x
                yb[at, tl] += jnp.sum(x, axis=0)
                return x

            lax.fori_loop(0, steps, step, carry, unroll=4)

        mixing = (qp[:, sl] * yb[:, sl]).astype(jnp.bfloat16)
        mix[here, c] = jnp.dot(
            perm_back[...], mixing, preferred_element_type=jnp.float32
        ).astype(jnp.bfloat16)

        @pl.when(has_right)
        def _():
            mix_copy(here, c, 1).start()

        @pl.when(has_left)
        def _():
            mix_copy(here, c, 0).start()

    for c in range(chunks + AHEAD):
        if c < chunks:
            local(c)
        if c >= AHEAD:
            finish(c - AHEAD)

    root = me * groups // ctx_count
    first_col = lax.rem(me * groups, ctx_count) * (channels // ctx_count)

    def final_copy(peer):
        return pltpu.make_async_remote_copy(
            src_ref=final_row.at[:, pl.ds(pl.multiple_of(first_col + peer * fin_stride, LANES), fin_width)],
            dst_ref=final_got,
            send_sem=fin_send.at[peer],
            recv_sem=fin_recv,
            device_id={"ch": peer},
            device_id_type=MESH,
        )

    @pl.when(here == root)
    def _():
        for d in range(1, groups):
            final_copy(lax.rem(here + d, groups)).start()

    w_copy.wait()

    def project(owner, c):
        at = pl.multiple_of(c * chunk, chunk)
        return jnp.dot(
            mix[owner, c],
            wb[pl.ds(pl.multiple_of(owner * channels + at, chunk), chunk), :],
            preferred_element_type=jnp.float32,
        )

    acc[...] = project(here, 0)
    if chunks > 1:
        @pl.loop(1, chunks)
        def _(c):
            acc[...] += project(here, c)

    @pl.loop(0, (groups - 1) * chunks)
    def _(n):
        d = 1 + n // chunks
        c = n % chunks
        left = here - d
        right = here + d

        @pl.when(left >= 0)
        def _():
            mix_copy(left, c, 1).wait_recv()

            @pl.when(has_right)
            def _():
                mix_copy(left, c, 1).start()

        @pl.when(right < groups)
        def _():
            mix_copy(right, c, 0).wait_recv()

            @pl.when(has_left)
            def _():
                mix_copy(right, c, 0).start()

        @pl.when(left >= 0)
        def _():
            acc[...] += project(left, c)

        @pl.when(right < groups)
        def _():
            acc[...] += project(right, c)

    out_ref[...] = acc[...].astype(jnp.bfloat16)

    @pl.when(here == root)
    def _():
        fin_ref[...] = final_row[:, pl.ds(pl.multiple_of(first_col + here * fin_stride, LANES), fin_width)]
        for d in range(1, groups):
            final_copy(lax.rem(here + d, groups)).wait_send()

    @pl.when(here != root)
    def _():
        final_copy(here).wait_recv()
        fin_ref[...] = final_got[...]

    for c in range(chunks):
        for d in range(1, ctx_count):
            state_copy(me, lax.rem(me + d, ctx_count), c).wait_send()

    @pl.loop(0, groups * chunks)
    def _(n):
        owner = n // chunks
        c = n % chunks

        @pl.when(jnp.logical_and(owner <= here, has_right))
        def _():
            mix_copy(owner, c, 1).wait_send()

        @pl.when(jnp.logical_and(owner >= here, has_left))
        def _():
            mix_copy(owner, c, 0).wait_send()


def write_out(out_ref, fin_ref, out_hbm, fin_hbm, sems):
    first = pltpu.make_async_copy(out_ref, out_hbm, sems.at[0])
    second = pltpu.make_async_copy(fin_ref, fin_hbm, sems.at[1])
    first.start()
    second.start()
    first.wait()
    second.wait()


def body(query_gate, key_gate, values, decay_rates, residues, skip_gain, out_weight):
    rows, channels = values.shape
    poles = decay_rates.shape[0]
    ctx_count = lax.axis_size("ctx")
    groups = lax.axis_size("ch")
    chunk = min(CHUNK, channels)
    chunks = channels // chunk
    columns = out_weight.shape[1]
    slice_width = channels // ctx_count
    aligned = slice_width % LANES == 0
    fin_width = slice_width if aligned else groups * slice_width
    fin_stride = slice_width if aligned else 0
    f32, bf16 = jnp.float32, jnp.bfloat16
    dma = pltpu.SemaphoreType.DMA
    any_spec = pl.BlockSpec(memory_space=pl.ANY)
    vmem = pl.BlockSpec(memory_space=pltpu.VMEM)
    layer_out, final = pl.pallas_call(
        functools.partial(kernel, ctx_count, groups, chunk, fin_width, fin_stride),
        out_shape=(
            jax.ShapeDtypeStruct((rows, columns), bf16),
            jax.ShapeDtypeStruct((poles, fin_width), f32),
        ),
        in_specs=[any_spec, any_spec, any_spec, vmem, vmem, vmem, any_spec],
        out_specs=(vmem, vmem),
        scratch_shapes=[
            pltpu.VMEM((rows, channels), bf16),
            pltpu.VMEM((rows, channels), bf16),
            pltpu.VMEM((rows, channels), bf16),
            pltpu.VMEM(out_weight.shape, bf16),
            pltpu.VMEM((rows, channels), f32),
            pltpu.VMEM((rows, channels), f32),
            pltpu.VMEM((rows, channels), f32),
            pltpu.VMEM((groups, chunks, rows, chunk), bf16),
            pltpu.VMEM((rows, columns), f32),
            pltpu.VMEM((ctx_count, chunks, poles, chunk), f32),
            pltpu.VMEM((poles, SEGS, channels), f32),
            pltpu.VMEM((poles, SEGS, channels), f32),
            pltpu.VMEM((poles, channels), f32),
            pltpu.VMEM((poles, channels), f32),
            pltpu.VMEM((poles, fin_width), f32),
            pltpu.VMEM((rows, rows), bf16),
            pltpu.VMEM((rows, rows), bf16),
            dma((3, chunks)),
            dma,
            dma((ctx_count, chunks)),
            dma((ctx_count, chunks)),
            dma((2, groups, chunks)),
            dma((groups, chunks)),
            dma((groups,)),
            dma,
        ],
        compiler_params=pltpu.CompilerParams(
            collective_id=0, has_side_effects=True, vmem_limit_bytes=60 * 1024 * 1024
        ),
    )(query_gate, key_gate, values, decay_rates, residues, skip_gain[None, :], out_weight)
    layer_out, final = pl.pallas_call(
        write_out,
        out_shape=(
            jax.ShapeDtypeStruct(layer_out.shape, layer_out.dtype),
            jax.ShapeDtypeStruct(final.shape, final.dtype),
        ),
        in_specs=[vmem, vmem],
        out_specs=(any_spec, any_spec),
        scratch_shapes=[dma((2,))],
    )(layer_out, final)
    if not aligned:
        final = lax.dynamic_slice_in_dim(final, lax.axis_index("ch") * slice_width, slice_width, 1)
    return layer_out, final


def solution(mesh):
    return jax.shard_map(
        body,
        mesh=mesh,
        in_specs=(
            P("ctx", "ch"),
            P("ctx", "ch"),
            P("ctx", "ch"),
            P(None, "ch"),
            P(None, "ch"),
            P("ch"),
            P(None, "ch"),
        ),
        out_specs=(P("ctx", "ch"), P(None, ("ctx", "ch"))),
        check_vma=False,
    )
```
